32 devices in a mesh: row: 4 (over y, x), col: 8 (over z, core).
Axes of the slice: x: 2, y: 2, z: 4, core: 2. Of those that a mesh axis runs over, the one named last changes fastest.
Arguments:
- anc_inverse: float32 [10240, 10240], P('row', 'col'), may hold values from -0.0625 to 0.0625
- lower_anc: float32 [10240, 3, 384], P('col', None, 'row'), may hold values from -1.5 to 1.5
- upper_anc: float32 [10240, 3, 384], P('row', None, 'col'), may hold values from -0.75 to 0.75
- lower_edge: float32 [2, 384, 384], replicated, may hold values from -0.3125 to 0.3125
- upper_edge: float32 [2, 384, 384], replicated, may hold values from -0.3125 to 0.3125
- diag_inverse: float32 [3, 384, 384], replicated, may hold values from -6 to 6
- tile_mask: int32 [3, 80, 3], replicated, may hold values 0 or 1
Outputs:
- x_blocks: float32 [10240, 3, 384], P(('row', 'col'))
- y_blocks: float32 [8, 4, 320, 3, 384], P('col', 'row')
- z_blocks: float32 [3, 384, 384], P(None, 'row', 'col')
- cross_blocks: float32 [2, 2, 384, 384], P(None, None, 'row', 'col')
The draws below stay inside these ranges and needn't reach their ends.
All inputs are finite; a program needn't handle non-finite values.
Results may differ from the reference program's by a relative error of at most 0.0001.
Values sent between devices are 32-bit elements; how exact they have to be, the bound alone decides.
A program may use at most 128 MiB of HBM per device.

```python
import jax
import jax.numpy as jnp
from jax import lax

ANC = 10240
W = 384
BLK = 128
SUPER = 3
EDGES = 2
NBLK = 80
WB = 3
PROW = 4
PCOL = 8
SLAB = 320


def with_ends(entries, stream_key, smallest, high):
    dims = entries.shape
    spot = [jax.random.randint(jax.random.fold_in(stream_key, axis), (), 0, dims[axis]) for axis in range(len(dims))]
    entries = entries.at[tuple(spot)].set(smallest)
    longest = dims.index(max(dims))
    spot[longest] = (spot[longest] + 1) % dims[longest]
    return entries.at[tuple(spot)].set(high)


def level_of(rng, shape, shards, low, largest):
    loudness = 1.0
    for dim, blocks in shards:
        steps = jax.random.uniform(jax.random.fold_in(jax.random.fold_in(rng, 6), dim), (blocks,), jnp.float32, low / len(shards), largest / len(shards))
        loudness = loudness * jnp.repeat(jnp.exp(steps), shape[dim] // blocks).reshape((-1,) + (1,) * (len(shape) - 1 - dim))
    return loudness


def gaussian(rng, dims, width, most, shards=(), held_as=jnp.bfloat16):
    array = jax.random.normal(rng, dims, jnp.float32) * width
    if len(shards) > 0:
        array = level_of(rng, dims, shards, -0.22, 0.18) * array
    return jnp.clip(array, min=-most, max=most).astype(held_as)


def setup_inputs(seed: int = 0) -> dict:
    seeds = jax.random.split(jax.random.key(seed), 8)
    anc_inverse = gaussian(seeds[0], (ANC, ANC), ANC ** -0.5, 0.0625, ((0, 4), (1, 8)), jnp.float32)
    lower_anc = gaussian(seeds[1], (ANC, SUPER, W), 0.25, 1.5, ((0, 8), (2, 4)), jnp.float32)
    upper_anc = gaussian(seeds[2], (ANC, SUPER, W), 0.125, 0.75, ((0, 4), (2, 8)), jnp.float32)
    lower_edge = gaussian(seeds[3], (EDGES, W, W), W ** -0.5, 0.3125, (), jnp.float32)
    upper_edge = gaussian(seeds[4], (EDGES, W, W), W ** -0.5, 0.3125, (), jnp.float32)
    diag_inverse = gaussian(seeds[5], (SUPER, W, W), 1.0, 6.0, (), jnp.float32)
    tile_mask = with_ends((jax.random.randint(seeds[6], (SUPER, NBLK, WB), 0, 4) < 3).astype(jnp.int32), jax.random.fold_in(seeds[6], 1), 0, 1)
    return {"anc_inverse": anc_inverse, "lower_anc": lower_anc, "upper_anc": upper_anc, "lower_edge": lower_edge, "upper_edge": upper_edge, "diag_inverse": diag_inverse, "tile_mask": tile_mask}


precise = lax.Precision.HIGHEST


def product(left, right):
    return jnp.dot(left, right, precision=precise, preferred_element_type=jnp.float32)


def expand_tiles(mask_rows):
    filled = mask_rows.astype(jnp.float32)
    return jnp.repeat(jnp.repeat(filled, BLK, axis=0), BLK, axis=1)


def reference(anc_inverse, lower_anc, upper_anc, lower_edge, upper_edge, diag_inverse, tile_mask):
    cols_list = []
    rows_list = []
    corner_list = []
    cross_cols = []
    cross_rows = []
    for node_index in range(SUPER):
        pattern = expand_tiles(tile_mask[node_index])
        lower_cur = lower_anc[:, node_index, :] * pattern
        upper_cur = upper_anc[:, node_index, :] * pattern
        inv_cols = -product(anc_inverse, lower_cur)
        inv_rows = -product(upper_cur.T, anc_inverse).T
        if node_index > 0:
            lower_side = lower_edge[node_index - 1]
            upper_side = upper_edge[node_index - 1]
            prev_cols = cols_list[-1]
            prev_rows = rows_list[-1]
            prev_corner = corner_list[-1]
            cross_col = -(product(prev_rows.T, lower_cur) + product(prev_corner, lower_side))
            cross_row = -(product(upper_cur.T, prev_cols) + product(upper_side, prev_corner))
            inv_cols = inv_cols - product(prev_cols, lower_side)
            inv_rows = inv_rows - product(prev_rows, upper_side.T)
            inv_corner = diag_inverse[node_index] - product(upper_cur.T, inv_cols) - product(upper_side, cross_col)
            cross_cols.append(cross_col)
            cross_rows.append(cross_row)
        else:
            inv_corner = diag_inverse[node_index] - product(upper_cur.T, inv_cols)
        cols_list.append(inv_cols)
        rows_list.append(inv_rows)
        corner_list.append(inv_corner)
    x_blocks = jnp.stack(cols_list, axis=1)
    y_blocks = jnp.stack(rows_list, axis=1).reshape(PCOL, PROW, SLAB, SUPER, W)
    z_blocks = jnp.stack(corner_list)
    cross_blocks = jnp.stack([jnp.stack(cross_cols), jnp.stack(cross_rows)])
    return x_blocks, y_blocks, z_blocks, cross_blocks
```

```python
import jax
import jax.numpy as jnp
from jax import lax
from jax.sharding import PartitionSpec as P


precise = lax.Precision.HIGH


def contract(left, right, left_dim, right_dim):
    return lax.dot_general(
        left,
        right,
        (((left_dim,), (right_dim,)), ((), ())),
        precision=precise,
        preferred_element_type=jnp.float32,
    )


def partner(index, step, count):
    if count & (count - 1) == 0:
        return index ^ step
    return (step - index) % count


def exchange(piece_for, axis):
    count = lax.axis_size(axis)
    index = lax.axis_index(axis)
    got = []
    for step in range(count):
        peer = partner(index, step, count)
        piece = piece_for(peer)
        pairs = [(i, partner(i, step, count)) for i in range(count)]
        if any(i != j for i, j in pairs):
            piece = lax.ppermute(piece, axis, pairs)
        got.append((peer, piece))
    return got


def mask_factor(factor, tile_mask, first_row, first_col, blk):
    rows, supers, cols = factor.shape
    blocks = rows // blk
    window = lax.dynamic_slice_in_dim(tile_mask, first_row // blk, blocks, 1).astype(jnp.float32)
    tile_cols = window.shape[2]
    tile_of_col = (first_col + jnp.arange(cols)) // blk
    pick = (tile_of_col[None, :] == jnp.arange(tile_cols)[:, None]).astype(jnp.float32)
    chosen = sum(window[:, :, t, None] * pick[t] for t in range(tile_cols))
    chosen = jnp.transpose(chosen, (1, 0, 2))
    masked = factor.reshape(blocks, blk, supers, cols) * chosen[:, None]
    return jnp.transpose(masked.reshape(rows, supers, cols), (1, 2, 0))


def per_device(anc_inverse, lower_anc, upper_anc, lower_edge, upper_edge, diag_inverse, tile_mask):
    rows_here, cols_here = anc_inverse.shape
    prow = lax.axis_size("row")
    pcol = lax.axis_size("col")
    supers, width = diag_inverse.shape[0], diag_inverse.shape[1]
    blk = width // tile_mask.shape[2]
    slab = rows_here // pcol
    row = lax.axis_index("row")
    col = lax.axis_index("col")
    part_lower = width // prow
    part_upper = width // pcol

    upper_t = mask_factor(upper_anc, tile_mask, row * rows_here, col * part_upper, blk)
    lower_t = mask_factor(lower_anc, tile_mask, col * cols_here, row * part_lower, blk)

    upper_t = lax.all_gather(upper_t, "col", axis=0)
    lower_full = jnp.zeros((supers, prow, part_lower, cols_here), jnp.float32)
    for peer, piece in exchange(lambda _: lower_t, "row"):
        lower_full = lax.dynamic_update_slice(lower_full, piece[:, None], (0, peer, 0, 0))
    lower_full = lower_full.reshape(supers, width, cols_here)
    lower_comb = [-lower_full[0]]
    for s in range(1, supers):
        lower_comb.append(-lower_full[s] - contract(lower_edge[s - 1], lower_comb[-1], 0, 0))
    cols_part = contract(anc_inverse, jnp.concatenate(lower_comb, 0), 1, 1)

    upper_full = jnp.transpose(upper_t, (1, 0, 2, 3)).reshape(supers, width, rows_here)
    upper_comb = [-upper_full[0]]
    for s in range(1, supers):
        upper_comb.append(-upper_full[s] - contract(upper_edge[s - 1], upper_comb[-1], 1, 0))
    rows_part = contract(anc_inverse, jnp.concatenate(upper_comb, 0), 0, 1)

    cols_send = jnp.transpose(cols_part.reshape(pcol, slab, supers, width), (0, 2, 1, 3))
    cols_mine = lax.psum_scatter(cols_send, "col", scatter_dimension=0, tiled=False)

    first = jnp.logical_and(row == 0, col == 0)
    corner = []
    cross_cols = []
    cross_rows = []
    for s in range(supers):
        here = slice(s * width, (s + 1) * width)
        before = slice((s - 1) * width, s * width)
        if s > 0:
            both = contract(upper_full[s], cols_part[:, (s - 1) * width : (s + 1) * width], 1, 0)
            upper_prev, upper_here = both[:, :width], both[:, width:]
        else:
            upper_here = contract(upper_full[s], cols_part[:, here], 1, 0)
        now = jnp.where(first, diag_inverse[s], 0.0) - upper_here
        if s > 0:
            lower_prev = lax.dot_general(
                rows_part[:, before],
                lower_full[s],
                (((0,), (1,)), ((), ())),
                precision=precise,
                preferred_element_type=jnp.float32,
            )
            cross_col = -(lower_prev + contract(corner[-1], lower_edge[s - 1], 1, 0))
            cross_row = -(upper_prev + contract(upper_edge[s - 1], corner[-1], 1, 0))
            now = now - contract(upper_edge[s - 1], cross_col, 1, 0)
            cross_cols.append(cross_col)
            cross_rows.append(cross_row)
        corner.append(now)
    sums = jnp.stack(corner + cross_cols + cross_rows)
    count = sums.shape[0]

    row_slab = cols_here // prow
    rows_send = jnp.transpose(rows_part.reshape(prow, row_slab, supers, width), (0, 2, 1, 3))
    rows_mine = sum(
        piece
        for _, piece in exchange(
            lambda peer: lax.dynamic_index_in_dim(rows_send, peer, 0, keepdims=False), "row"
        )
    )
    sums, rows_mine = lax.optimization_barrier((sums, rows_mine))
    sums = sum(
        piece
        for _, piece in exchange(
            lambda peer: lax.dynamic_slice_in_dim(sums, peer * part_lower, part_lower, 1), "row"
        )
    )
    sums = jnp.transpose(sums.reshape(count * part_lower, width))
    sums, cols_mine = lax.optimization_barrier((sums, cols_mine))
    sums = lax.psum_scatter(sums, "col", scatter_dimension=0, tiled=True)
    sums = jnp.transpose(sums).reshape(count, part_lower, part_upper)

    x_blocks = jnp.transpose(cols_mine, (1, 0, 2))
    y_blocks = jnp.transpose(rows_mine, (1, 0, 2))[None, None]
    z_blocks = sums[:supers]
    cross_blocks = sums[supers:].reshape(2, supers - 1, part_lower, part_upper)
    return (x_blocks, y_blocks, z_blocks, cross_blocks)


def solution(mesh):
    return jax.shard_map(
        per_device,
        mesh=mesh,
        in_specs=(
            P("row", "col"),
            P("col", None, "row"),
            P("row", None, "col"),
            P(),
            P(),
            P(),
            P(),
        ),
        out_specs=(
            P(("row", "col"), None, None),
            P("col", "row", None, None, None),
            P(None, "row", "col"),
            P(None, None, "row", "col"),
        ),
        check_vma=False,
    )
```

```python
import jax
import jax.numpy as jnp
from jax import lax
from jax.experimental.layout import Layout, with_layout_constraint
from jax.sharding import PartitionSpec as P


precise = lax.Precision.HIGH


def contract(left, right, left_dim, right_dim):
    return lax.dot_general(
        left,
        right,
        (((left_dim,), (right_dim,)), ((), ())),
        precision=precise,
        preferred_element_type=jnp.float32,
    )


def row_major(array):
    return with_layout_constraint(array, Layout(major_to_minor=(0, 1)))


def partner(index, step, count):
    if count & (count - 1) == 0:
        return index ^ step
    return (step - index) % count


def exchange(piece_for, axis):
    count = lax.axis_size(axis)
    index = lax.axis_index(axis)
    got = []
    for step in range(count):
        peer = partner(index, step, count)
        piece = piece_for(peer)
        pairs = [(i, partner(i, step, count)) for i in range(count)]
        if any(i != j for i, j in pairs):
            piece = lax.ppermute(piece, axis, pairs)
        got.append((peer, piece))
    return got


def mask_factor(factor, tile_mask, first_row, first_col, blk):
    rows, supers, cols = factor.shape
    blocks = rows // blk
    window = lax.dynamic_slice_in_dim(tile_mask, first_row // blk, blocks, 1).astype(jnp.float32)
    tile_cols = window.shape[2]
    tile_of_col = (first_col + jnp.arange(cols)) // blk
    pick = (tile_of_col[None, :] == jnp.arange(tile_cols)[:, None]).astype(jnp.float32)
    chosen = sum(window[:, :, t, None] * pick[t] for t in range(tile_cols))
    chosen = jnp.transpose(chosen, (1, 0, 2))
    masked = factor.reshape(blocks, blk, supers, cols) * chosen[:, None]
    return jnp.transpose(masked.reshape(rows, supers, cols), (1, 2, 0))


def per_device(anc_inverse, lower_anc, upper_anc, lower_edge, upper_edge, diag_inverse, tile_mask):
    rows_here, cols_here = anc_inverse.shape
    prow = lax.axis_size("row")
    pcol = lax.axis_size("col")
    supers, width = diag_inverse.shape[0], diag_inverse.shape[1]
    blk = width // tile_mask.shape[2]
    row = lax.axis_index("row")
    col = lax.axis_index("col")
    part_lower = width // prow
    part_upper = width // pcol

    upper_t = mask_factor(upper_anc, tile_mask, row * rows_here, col * part_upper, blk)
    lower_t = mask_factor(lower_anc, tile_mask, col * cols_here, row * part_lower, blk)

    upper_t = lax.all_gather(upper_t, "col", axis=0)
    lower_full = jnp.zeros((supers, prow, part_lower, cols_here), jnp.float32)
    for peer, piece in exchange(lambda _: lower_t, "row"):
        lower_full = lax.dynamic_update_slice(lower_full, piece[:, None], (0, peer, 0, 0))
    lower_full = lower_full.reshape(supers, width, cols_here)
    lower_comb = [-lower_full[0]]
    for s in range(1, supers):
        lower_comb.append(-lower_full[s] - contract(lower_edge[s - 1], lower_comb[-1], 0, 0))
    cols_part = [row_major(contract(anc_inverse, one, 1, 1)) for one in lower_comb]
    cols_mine = [lax.psum_scatter(one, "col", scatter_dimension=0, tiled=True) for one in cols_part]

    upper_full = [upper_t[:, s].reshape(width, rows_here) for s in range(supers)]
    upper_comb = [-upper_full[0]]
    for s in range(1, supers):
        upper_comb.append(-upper_full[s] - contract(upper_edge[s - 1], upper_comb[-1], 1, 0))
    rows_part = [row_major(contract(anc_inverse, one, 0, 1)) for one in upper_comb]

    first = jnp.logical_and(row == 0, col == 0)
    corner = []
    cross_cols = []
    cross_rows = []
    for s in range(supers):
        upper_here = contract(upper_full[s], cols_part[s], 1, 0)
        now = jnp.where(first, diag_inverse[s], 0.0) - upper_here
        if s > 0:
            upper_prev = contract(upper_full[s], cols_part[s - 1], 1, 0)
            lower_prev = lax.dot_general(
                rows_part[s - 1],
                lower_full[s],
                (((0,), (1,)), ((), ())),
                precision=precise,
                preferred_element_type=jnp.float32,
            )
            cross_col = -(lower_prev + contract(corner[-1], lower_edge[s - 1], 1, 0))
            cross_row = -(upper_prev + contract(upper_edge[s - 1], corner[-1], 1, 0))
            now = now - contract(upper_edge[s - 1], cross_col, 1, 0)
            cross_cols.append(cross_col)
            cross_rows.append(cross_row)
        corner.append(now)
    sums = jnp.stack(corner + cross_cols + cross_rows)
    count = sums.shape[0]

    row_slab = cols_here // prow
    rows_mine = [
        sum(
            piece
            for _, piece in exchange(
                lambda peer: lax.dynamic_slice_in_dim(one, peer * row_slab, row_slab, 0), "row"
            )
        )
        for one in rows_part
    ]
    sums, rows_mine = lax.optimization_barrier((sums, rows_mine))
    sums = sum(
        piece
        for _, piece in exchange(
            lambda peer: lax.dynamic_slice_in_dim(sums, peer * part_lower, part_lower, 1), "row"
        )
    )
    sums = jnp.transpose(sums.reshape(count * part_lower, width))
    sums, cols_mine = lax.optimization_barrier((sums, cols_mine))
    sums = lax.psum_scatter(sums, "col", scatter_dimension=0, tiled=True)
    sums = jnp.transpose(sums).reshape(count, part_lower, part_upper)

    x_blocks = jnp.stack(cols_mine, axis=1)
    y_blocks = jnp.stack(rows_mine, axis=1)[None, None]
    z_blocks = sums[:supers]
    cross_blocks = sums[supers:].reshape(2, supers - 1, part_lower, part_upper)
    return (x_blocks, y_blocks, z_blocks, cross_blocks)


def solution(mesh):
    return jax.shard_map(
        per_device,
        mesh=mesh,
        in_specs=(
            P("row", "col"),
            P("col", None, "row"),
            P("row", None, "col"),
            P(),
            P(),
            P(),
            P(),
        ),
        out_specs=(
            P(("row", "col"), None, None),
            P("col", "row", None, None, None),
            P(None, "row", "col"),
            P(None, None, "row", "col"),
        ),
        check_vma=False,
    )
```
